32 devices in a mesh: expert: 16 (over z, x, core), tensor: 2 (over y).
Axes of the slice: x: 2, y: 2, z: 4, core: 2. Of those that a mesh axis runs over, the one named last changes fastest.
Arguments:
- tokens: bfloat16 [256, 7168], P('expert', 'tensor'), may hold values from -6 to 6
- expert_ids: int32 [256, 8], P('expert'), may hold values from 0 to 7, as said below
- route_weights: float32 [256, 8], P('expert'), may hold values from 0.05 to 1
- gate_weight: bfloat16 [16, 512, 7168], P('expert', 'tensor'), may hold values from -0.0625 to 0.0625
- up_weight: bfloat16 [16, 512, 7168], P('expert', 'tensor'), may hold values from -0.0625 to 0.0625
- down_weight: bfloat16 [16, 512, 7168], P('expert', 'tensor'), may hold values from -0.1875 to 0.1875
Outputs:
- mixed: bfloat16 [256, 7168], P('expert', 'tensor')
The draws below stay inside these ranges and needn't reach their ends.
Inputs may be any that keep to these rules, and one draw needn't show every extreme that they name: `expert_ids`: each row holds 8 different experts. One expert, the same for all tokens, is named by exactly 16 of the 16 tokens of every block of 16 consecutive tokens; every other expert by at most 16 tokens of a block.
All inputs are finite; a program needn't handle non-finite values.
Results may differ from the reference program's by a relative error of at most 0.015.
Values may be sent and summed in bfloat16 or wider, within the bound.
A program may use at most 64 MiB of HBM per device.

```python
import math
import jax
import jax.numpy as jnp
from jax import lax

D = 7168
TOP = 8
FF = 1024
TOK_DEV = 16
EXPERTS = 8
TOKENS = 256
CAP = 16
N_TENSOR = 2


def draw_expert_ids(key, part):
    hot_expert = jax.random.randint(jax.random.fold_in(key, 7), (), 0, EXPERTS)
    block_keys = jax.random.split(jax.random.fold_in(key, 11), TOKENS // TOK_DEV)
    column = jnp.arange(TOP, dtype=jnp.int32)

    def one_block(block_key):
        key_order = jax.random.fold_in(block_key, 1)
        key_others = jax.random.fold_in(block_key, 2)
        key_columns = jax.random.fold_in(block_key, 3)
        position = jax.random.permutation(key_order, TOK_DEV).astype(jnp.int32)
        others = jax.random.permutation(key_others, EXPERTS - 1).astype(jnp.int32)
        others = others + (others >= hot_expert).astype(jnp.int32)
        is_hot = position < CAP
        offset = jnp.where(is_hot, position * (TOP - 1), CAP * (TOP - 1) + (position - CAP) * TOP)
        shifted = is_hot.astype(jnp.int32)
        index_table = jnp.mod(offset[:, None] + column[None, :] - shifted[:, None], EXPERTS - 1)
        rows = others[index_table]
        rows = jnp.where(is_hot[:, None] & (column[None, :] == 0), hot_expert, rows)
        scores = jax.random.randint(key_columns, (TOK_DEV, TOP), 0, 1 << 20) * TOP + column[None, :]
        order = jnp.argsort(scores, axis=1)
        return jnp.take_along_axis(rows, order, axis=1)
    result = jax.vmap(one_block)(block_keys)
    return result.reshape(TOKENS, TOP).astype(jnp.int32)


def block_scale(stream_key, dims, pieces, smallest, top_value):
    level, own = 1.0, jax.random.fold_in(stream_key, 6)
    for dim, parts in pieces:
        heights = jnp.exp(jax.random.uniform(jax.random.fold_in(own, dim), (parts,), jnp.float32, smallest / len(pieces), top_value / len(pieces)))
        level = level * jnp.repeat(heights, dims[dim] // parts).reshape([-1 if axis == dim else 1 for axis in range(len(dims))])
    return level


def noise(stream_key, dims, width, limit, cuts=(), held_as=jnp.bfloat16):
    values = jax.random.normal(stream_key, dims, jnp.float32) * width
    if len(cuts) > 0:
        values = block_scale(stream_key, dims, cuts, -0.22, 0.18) * values
    return jnp.clip(values, min=-limit, max=limit).astype(held_as)


def setup_inputs(seed: int = 0) -> dict:
    key_of = jax.random.split(jax.random.key(seed), 7)
    return {
        "tokens": noise(key_of[0], (TOKENS, D), 1.0, 6.0, ((0, 16), (1, 2))),
        "expert_ids": draw_expert_ids(jax.random.fold_in(key_of[6], 71), 0),
        "route_weights": jnp.clip(jnp.exp(math.log(1.0) - 2.9957323 * jax.random.uniform(key_of[2], (TOKENS, TOP), jnp.float32) ** block_scale(key_of[2], (TOKENS, TOP), ((0, 16),), -0.2, 0.2)), 0.05, 1.0),
        "gate_weight": noise(key_of[3], (2 * EXPERTS, FF // 2, D), D ** -0.5, 0.0625, ((0, 16), (1, 2))),
        "up_weight": noise(key_of[4], (2 * EXPERTS, FF // 2, D), D ** -0.5, 0.0625, ((0, 16), (1, 2))),
        "down_weight": noise(key_of[5], (2 * EXPERTS, FF // 2, D), FF ** -0.5, 0.1875, ((0, 16), (1, 2))),
    }


def reference(tokens, expert_ids, route_weights, gate_weight, up_weight, down_weight):
    block_count = TOKENS // TOK_DEV
    slot_count = block_count * CAP
    unit_count = FF // (2 * N_TENSOR)
    expert_range = jnp.arange(EXPERTS, dtype=jnp.int32)
    onehot = jnp.sum((expert_ids[:, :, None] == expert_range[None, None, :]).astype(jnp.int32), axis=1)
    onehot_blocks = onehot.reshape(block_count, TOK_DEV, EXPERTS)
    earlier_count = (jnp.cumsum(onehot_blocks, axis=1) - onehot_blocks).reshape(TOKENS, EXPERTS)
    slot_rank = jnp.take_along_axis(earlier_count, expert_ids, axis=1)
    token_range = jnp.arange(TOKENS, dtype=jnp.int32)
    slot_index = (token_range // TOK_DEV)[:, None] * CAP + slot_rank
    token_table = jnp.full((EXPERTS, slot_count), TOKENS, dtype=jnp.int32)
    token_table = token_table.at[expert_ids, slot_index].set(jnp.broadcast_to(token_range[:, None], expert_ids.shape))
    padded = jnp.concatenate([tokens, jnp.zeros((1, D), jnp.bfloat16)], axis=0)

    def run_expert(expert):
        expert_rows = padded[token_table[expert]]
        halves = []
        for half in range(2):
            entry = 2 * expert + half
            gate_act = jnp.dot(expert_rows, gate_weight[entry].T, preferred_element_type=jnp.float32)
            up_act = jnp.dot(expert_rows, up_weight[entry].T, preferred_element_type=jnp.float32)
            hidden = (jax.nn.silu(gate_act) * up_act).astype(jnp.bfloat16)
            hidden_groups = hidden.reshape(slot_count, N_TENSOR, unit_count).astype(jnp.float32)
            down_groups = down_weight[entry].reshape(N_TENSOR, unit_count, D).astype(jnp.float32)
            group_terms = jnp.einsum("rgf,gfd->grd", hidden_groups, down_groups).astype(jnp.bfloat16)
            group_terms = lax.optimization_barrier(group_terms)
            halves.append(jnp.sum(group_terms.astype(jnp.float32), axis=0).astype(jnp.bfloat16))
        return jnp.stack(halves, axis=0)

    half_out = lax.map(run_expert, expert_range)
    picked = half_out[expert_ids, 0, slot_index].astype(jnp.float32) + half_out[expert_ids, 1, slot_index].astype(jnp.float32)
    mixed = jnp.sum(route_weights[:, :, None] * picked, axis=1)
    return mixed.astype(jnp.bfloat16)
```

```python
import functools

import jax
import jax.numpy as jnp
from jax import lax
from jax.experimental import pallas as pl
from jax.experimental.pallas import tpu as pltpu
from jax.sharding import PartitionSpec as P

LANES = 128


def rows_times(rows, weight):
    return lax.dot_general(
        rows, weight, (((1,), (1,)), ((), ())), preferred_element_type=jnp.float32
    )


def sparse_body(tokens, expert_ids, route_weights, gate_weight, up_weight, down_weight):
    devices_wide = lax.axis_size("expert")
    experts = devices_wide // 2
    tok_count = expert_ids.shape[0]
    per_token = expert_ids.shape[1]
    capacity = min(tok_count, tok_count * per_token // experts)
    slot_count = experts * capacity
    arrived_count = devices_wide * capacity
    expert_range = jnp.arange(experts, dtype=jnp.int32)
    onehot = jnp.sum(
        (expert_ids[:, :, None] == expert_range[None, None, :]).astype(jnp.int32), axis=1
    )
    earlier_count = jnp.cumsum(onehot, axis=0) - onehot
    slot_rank = jnp.take_along_axis(earlier_count, expert_ids, axis=1)
    slot_of = expert_ids * capacity + slot_rank
    slot_range = jnp.arange(slot_count, dtype=jnp.int32)
    select = jnp.any(slot_of[None, :, :] == slot_range[:, None, None], axis=2).astype(jnp.bfloat16)
    weight_gate = gate_weight[0]
    weight_up = up_weight[0]
    weight_out = down_weight[0]
    whole_rows = lax.all_gather(tokens, "tensor", axis=1, tiled=True)
    packed = jnp.dot(select, whole_rows, preferred_element_type=jnp.float32).astype(jnp.bfloat16)
    packed = packed.reshape(experts, capacity, whole_rows.shape[1])
    arrived = lax.all_to_all(
        jnp.repeat(packed, 2, axis=0), "expert", split_axis=0, concat_axis=0, tiled=True
    ).reshape(arrived_count, -1)
    gate_act = rows_times(arrived, weight_gate)
    up_act = rows_times(arrived, weight_up)
    hidden = (jax.nn.silu(gate_act) * up_act).astype(jnp.bfloat16)
    columns = lax.all_to_all(weight_out, "tensor", split_axis=1, concat_axis=0, tiled=True)
    unit_count = hidden.shape[1]
    shard_piece = lax.all_gather(hidden, "tensor", axis=1, tiled=True)
    groups = shard_piece.shape[1] // unit_count
    weight_rows = columns
    weight_rows = weight_rows.reshape(groups, unit_count, columns.shape[1])
    grouped = shard_piece.reshape(shard_piece.shape[0], groups, unit_count)
    group_terms = jnp.einsum(
        "rgf,gfd->grd", grouped, weight_rows, preferred_element_type=jnp.float32
    ).astype(jnp.bfloat16)
    group_terms = lax.optimization_barrier(group_terms)
    half_out = jnp.sum(group_terms.astype(jnp.float32), axis=0).astype(jnp.bfloat16)
    returned = lax.all_to_all(
        half_out.reshape(devices_wide, capacity, -1),
        "expert",
        split_axis=0,
        concat_axis=0,
        tiled=True,
    )
    returned = returned.reshape(experts, 2, capacity, -1).astype(jnp.float32)
    combined = (returned[:, 0] + returned[:, 1]).reshape(slot_count, -1)
    picked = combined[slot_of]
    mixed_out = jnp.sum(route_weights[:, :, None] * picked, axis=1)
    return mixed_out.astype(jnp.bfloat16)


def fused_kernel(
    nz, tok_ref, ids_ref, rw_ref, gate_hbm, up_hbm, down_hbm, out_ref,
    rows_a, rows_b, gate, up, down, part, core_buf, x_buf, y_buf, z_buf, acc,
    load_sem, row_sem, az_send, ax_send, ay_send, ac_send,
    core_send, core_recv, x_send, x_recv, y_send, y_recv, z_send, z_recv,
):
    me, y = lax.axis_index("expert"), lax.axis_index("tensor")
    c = lax.rem(me, 2)
    x = lax.rem(me // 2, 2)
    z = me // 4
    oc, ox, oy = 1 - c, 1 - x, 1 - y
    tok, wide = out_ref.shape
    half = wide // 2
    blocks = 2 * nz
    count = 2 * blocks * tok
    experts = blocks
    top = ids_ref.shape[1]
    rows = (rows_a, rows_b)

    def dev(zz, xx, cc, yy):
        return ((zz * 2 + xx) * 2 + cc, yy)

    above, below = dev(z + 1, x, c, y), dev(z - 1, x, c, y)
    dev_x, dev_y, dev_c = dev(z, ox, c, y), dev(z, x, c, oy), dev(z, x, oc, y)
    has_above, has_below = z < nz - 1, z > 0

    def remote(src, dst, send, recv, to):
        return pltpu.make_async_remote_copy(
            src_ref=src, dst_ref=dst, send_sem=send, recv_sem=recv,
            device_id=to, device_id_type=pl.DeviceIdType.MESH,
        )

    loads = [
        pltpu.make_async_copy(src.at[0], dst, load_sem.at[i])
        for i, (src, dst) in enumerate(((gate_hbm, gate), (up_hbm, up), (down_hbm, down)))
    ]
    for load in loads:
        load.start()

    own = x * nz + z
    lane = lax.broadcasted_iota(jnp.int32, (tok, LANES), 1)
    which = lax.rem(lane, experts)
    spread = jnp.zeros((tok, LANES), jnp.float32)
    for j in range(top):
        spread = jnp.where(ids_ref[:, j : j + 1] == which, rw_ref[:, j : j + 1], spread)
    first = spread.astype(jnp.bfloat16).astype(jnp.float32)
    rest = spread - first
    second = rest.astype(jnp.bfloat16).astype(jnp.float32)
    third = rest - second
    parts = jnp.where(lane < experts, first, jnp.where(lane < 2 * experts, second, third))
    parts = jnp.where(lane < 3 * experts, parts, 0.0)
    rows_a[y, c, own, :, :half] = tok_ref[:, :half]
    rows_a[y, c, own, :, half:] = parts.astype(jnp.bfloat16)
    rows_b[y, c, own] = tok_ref[:, half:]

    barrier = pltpu.get_barrier_semaphore()
    for to in (dev_x, dev_y, dev_c):
        pl.semaphore_signal(barrier, inc=1, device_id=to, device_id_type=pl.DeviceIdType.MESH)

    @pl.when(has_above)
    def _():
        pl.semaphore_signal(barrier, inc=1, device_id=above, device_id_type=pl.DeviceIdType.MESH)

    @pl.when(has_below)
    def _():
        pl.semaphore_signal(barrier, inc=1, device_id=below, device_id_type=pl.DeviceIdType.MESH)

    pl.semaphore_wait(barrier, 3 + has_above.astype(jnp.int32) + has_below.astype(jnp.int32))

    def row_copy(h, yy, cc, xx, zz, send, to):
        at = (yy, cc, xx * nz + zz)
        return remote(rows[h].at[at], rows[h].at[at], send, row_sem.at[(h,) + at], to)

    def got(h, yy, xx, zz):
        row_copy(h, yy, c, xx, zz, ac_send.at[h, yy, xx * nz + zz], dev_c).wait_recv()

    def z_copy(h, zz, way):
        return row_copy(h, y, c, x, zz, az_send.at[way, h, zz], above if way else below)

    def x_copy(h, yy, zz):
        return row_copy(h, yy, c, x, zz, ax_send.at[h, yy, zz], dev_x)

    def y_copy(h, xx, zz):
        return row_copy(h, y, c, xx, zz, ay_send.at[h, xx, zz], dev_y)

    def c_copy(h, yy, xx, zz):
        return row_copy(h, yy, c, xx, zz, ac_send.at[h, yy, xx * nz + zz], dev_c)

    def start_up(h, zz):
        @pl.when(has_above)
        def _():
            z_copy(h, zz, 1).start()

    def start_down(h, zz):
        @pl.when(has_below)
        def _():
            z_copy(h, zz, 0).start()

    def column_sends(zz):
        x_copy(0, y, zz).start()
        y_copy(1, x, zz).start()
        y_copy(0, x, zz).start()
        x_copy(1, y, zz).start()
        c_copy(0, y, x, zz).start()
        c_copy(1, y, x, zz).start()

    def near_first(k):
        return jnp.where(z < nz // 2, k, nz - 1 - k)

    for h in range(2):
        start_up(h, z)
        start_down(h, z)
    column_sends(z)

    def gather_step(k, carry):
        zz = near_first(k)

        @pl.when(zz < z)
        def _():
            for h in range(2):
                got(h, y, x, zz)
                start_up(h, zz)

        @pl.when(zz > z)
        def _():
            for h in range(2):
                got(h, y, x, zz)
                start_down(h, zz)

        @pl.when(zz != z)
        def _():
            column_sends(zz)

        got(0, y, ox, zz)
        y_copy(0, ox, zz).start()
        c_copy(0, y, ox, zz).start()
        got(1, oy, x, zz)
        x_copy(1, oy, zz).start()
        c_copy(1, oy, x, zz).start()
        return carry

    lax.fori_loop(0, nz, gather_step, 0)

    def last_step(k, carry):
        zz = near_first(k)
        for h, yy, xx in ((0, oy, x), (1, y, ox), (0, oy, ox), (1, oy, ox)):
            got(h, yy, xx, zz)
            c_copy(h, yy, xx, zz).start()
        return carry

    lax.fori_loop(0, nz, last_step, 0)

    def from_core(k, carry):
        for h in range(2):
            for yy in range(2):
                at = (yy, oc, k)
                remote(
                    rows[h].at[at], rows[h].at[at], ac_send.at[h, yy, k], row_sem.at[(h,) + at], dev_c
                ).wait_recv()
        return carry

    lax.fori_loop(0, blocks, from_core, 0)
    loads[0].wait()
    loads[1].wait()

    contract = (((1,), (1,)), ((), ()))
    gate_act = up_act = None
    for yy in range(2):
        for h in range(2):
            block = rows[h][yy, :, :, :, :half].reshape(count, half)
            cols = slice((2 * yy + h) * half, (2 * yy + h + 1) * half)
            g = lax.dot_general(block, gate[:, cols], contract, preferred_element_type=jnp.float32)
            u = lax.dot_general(block, up[:, cols], contract, preferred_element_type=jnp.float32)
            gate_act = g if gate_act is None else gate_act + g
            up_act = u if up_act is None else up_act + u
    lanes = lax.broadcasted_iota(jnp.int32, (count, LANES), 1)
    mine = (lax.rem(lanes, experts) == me // 2) & (lanes < 3 * experts)
    kept = rows_a[0, :, :, :, half:].reshape(count, LANES).astype(jnp.float32)
    scale = jnp.sum(jnp.where(mine, kept, 0.0), axis=1, keepdims=True)
    hidden = (jax.nn.silu(gate_act) * up_act * scale).astype(jnp.bfloat16)
    loads[2].wait()

    def core_copy(yy, h):
        return remote(
            part.at[yy, h, oc], core_buf.at[yy, h], core_send.at[yy, h], core_recv.at[yy, h], dev_c
        )

    order = ((oy, 0), (oy, 1), (y, 1), (y, 0))
    for yy, h in order:
        base = (2 * yy + h) * half
        piece = 256

        def down_step(k, carry):
            cols = pl.ds(pl.multiple_of(base + k * piece, 128), piece)
            got_cols = pl.ds(pl.multiple_of(k * piece, 128), piece)
            term = jnp.dot(hidden, down[:, cols], preferred_element_type=jnp.float32)
            part[yy, h, :, :, :, got_cols] = term.astype(jnp.bfloat16).reshape(2, blocks, tok, piece)
            return carry

        lax.fori_loop(0, half // piece, down_step, 0)
        core_copy(yy, h).start()

    def far_first(k):
        return jnp.where(z < nz // 2, nz - 1 - k, k)

    def rx(h, yy, zz):
        return remote(
            part.at[yy, h, c, ox * nz + zz], x_buf.at[h, yy, zz], x_send.at[h, yy, zz], x_recv.at[h, yy, zz], dev_x
        )

    def ry(h, xx, zz):
        return remote(
            part.at[oy, h, c, xx * nz + zz], y_buf.at[h, xx, zz], y_send.at[h, xx, zz], y_recv.at[h, xx, zz], dev_y
        )

    def rz(h, zz, way):
        return remote(
            part.at[y, h, c, x * nz + zz], z_buf.at[way, h, zz], z_send.at[way, h, zz], z_recv.at[way, h, zz],
            above if way else below,
        )

    wide_f = jnp.float32
    for yy, h in order:
        core_copy(yy, h).wait_recv()

        def add_core(k, carry):
            total = part[yy, h, c, k].astype(wide_f) + core_buf[yy, h, k].astype(wide_f)
            part[yy, h, c, k] = total.astype(jnp.bfloat16)
            return carry

        lax.fori_loop(0, blocks, add_core, 0)

        def first_sends(k, carry):
            zz = far_first(k)
            if h == 0:
                ry(0, ox, zz).start()
                ry(0, x, zz).start()
            else:
                rx(1, yy, zz).start()
            return carry

        if (h == 0) == (yy is oy) or h == 1:
            lax.fori_loop(0, nz, first_sends, 0)

    def reduce_step(k, carry):
        zz = far_first(k)
        ry(0, ox, zz).wait_recv()
        at = x_of(ox, zz)
        part[y, 0, c, at] = (part[y, 0, c, at].astype(wide_f) + y_buf[0, ox, zz].astype(wide_f)).astype(jnp.bfloat16)
        rx(0, y, zz).start()
        rx(1, oy, zz).wait_recv()
        at = x_of(x, zz)
        part[oy, 1, c, at] = (part[oy, 1, c, at].astype(wide_f) + x_buf[1, oy, zz].astype(wide_f)).astype(jnp.bfloat16)
        ry(1, x, zz).start()
        return carry

    def x_of(xx, zz):
        return xx * nz + zz

    lax.fori_loop(0, nz, reduce_step, 0)

    def line_step(k, carry):
        zz = far_first(k)
        at = x_of(x, zz)
        for h in range(2):
            ry(h, x, zz).wait_recv()
            rx(h, y, zz).wait_recv()
            acc[...] = (
                part[y, h, c, at].astype(wide_f) + y_buf[h, x, zz].astype(wide_f) + x_buf[h, y, zz].astype(wide_f)
            )

            @pl.when((zz <= z) & has_above)
            def _():
                rz(h, zz, 0).wait_recv()
                acc[...] += z_buf[0, h, zz].astype(wide_f)

            @pl.when((zz >= z) & has_below)
            def _():
                rz(h, zz, 1).wait_recv()
                acc[...] += z_buf[1, h, zz].astype(wide_f)

            @pl.when(zz == z)
            def _():
                out_ref[:, h * half : (h + 1) * half] = acc[...].astype(jnp.bfloat16)

            @pl.when(zz != z)
            def _():
                part[y, h, c, at] = acc[...].astype(jnp.bfloat16)

            @pl.when(zz < z)
            def _():
                rz(h, zz, 0).start()

            @pl.when(zz > z)
            def _():
                rz(h, zz, 1).start()
        return carry

    lax.fori_loop(0, nz, line_step, 0)

    def drain(zz, carry):
        for h in range(2):
            @pl.when((zz <= z) & has_above)
            def _():
                z_copy(h, zz, 1).wait_send()

            @pl.when((zz >= z) & has_below)
            def _():
                z_copy(h, zz, 0).wait_send()

            @pl.when(zz < z)
            def _():
                rz(h, zz, 0).wait_send()

            @pl.when(zz > z)
            def _():
                rz(h, zz, 1).wait_send()

            for yy in range(2):
                for xx in range(2):
                    c_copy(h, yy, xx, zz).wait_send()
        x_copy(0, y, zz).wait_send()
        y_copy(1, x, zz).wait_send()
        rx(0, y, zz).wait_send()
        ry(1, x, zz).wait_send()
        for i in range(2):
            x_copy(1, i, zz).wait_send()
            y_copy(0, i, zz).wait_send()
            rx(1, i, zz).wait_send()
            ry(0, i, zz).wait_send()
        return carry

    lax.fori_loop(0, nz, drain, 0)
    for yy in range(2):
        for h in range(2):
            core_copy(yy, h).wait_send()


def fused_body(tokens, expert_ids, route_weights, gate_weight, up_weight, down_weight):
    nz = lax.axis_size("expert") // 4
    tok, wide = tokens.shape
    half = wide // 2
    blocks = 2 * nz
    bf16 = jnp.bfloat16
    held = gate_weight.shape[1:]
    vmem = pl.BlockSpec(memory_space=pltpu.VMEM)
    anywhere = pl.BlockSpec(memory_space=pl.ANY)
    sems = pltpu.SemaphoreType.DMA
    return pl.pallas_call(
        functools.partial(fused_kernel, nz),
        out_shape=jax.ShapeDtypeStruct((tok, wide), bf16),
        in_specs=[vmem] * 3 + [anywhere] * 3,
        out_specs=vmem,
        scratch_shapes=[
            pltpu.VMEM((2, 2, blocks, tok, half + LANES), bf16),
            pltpu.VMEM((2, 2, blocks, tok, half), bf16),
            pltpu.VMEM(held, bf16),
            pltpu.VMEM(held, bf16),
            pltpu.VMEM(held, bf16),
            pltpu.VMEM((2, 2, 2, blocks, tok, half), bf16),
            pltpu.VMEM((2, 2, blocks, tok, half), bf16),
            pltpu.VMEM((2, 2, nz, tok, half), bf16),
            pltpu.VMEM((2, 2, nz, tok, half), bf16),
            pltpu.VMEM((2, 2, nz, tok, half), bf16),
            pltpu.VMEM((tok, half), jnp.float32),
            sems((3,)),
            sems((2, 2, 2, blocks)),
            sems((2, 2, nz)),
            sems((2, 2, nz)),
            sems((2, 2, nz)),
            sems((2, 2, blocks)),
            sems((2, 2)),
            sems((2, 2)),
        ]
        + [sems((2, 2, nz))] * 6,
        compiler_params=pltpu.CompilerParams(
            collective_id=0, has_side_effects=True, vmem_limit_bytes=60 * 2**20
        ),
    )(tokens, expert_ids, route_weights, gate_weight, up_weight, down_weight)


def body(*args):
    every = args[1].shape[1] == lax.axis_size("expert") // 2
    tok, wide = args[0].shape
    even = lax.axis_size("tensor") == 2 and lax.axis_size("expert") % 8 == 0
    fits = tok % 16 == 0 and wide % 512 == 0 and 3 * args[1].shape[1] <= LANES
    if every and even and fits:
        return fused_body(*args)
    return sparse_body(*args)


def solution(mesh):
    placed = (
        P("expert", "tensor"),
        P("expert", None),
        P("expert", None),
        P("expert", "tensor", None),
        P("expert", "tensor", None),
        P("expert", "tensor", None),
    )
    return jax.shard_map(
        body, mesh=mesh, in_specs=placed, out_specs=P("expert", "tensor"), check_vma=False
    )
```

```python
import functools

import jax
import jax.numpy as jnp
from jax import lax
from jax.experimental import pallas as pl
from jax.experimental.pallas import tpu as pltpu
from jax.sharding import PartitionSpec as P

LANES = 128


def rows_times(rows, weight):
    return lax.dot_general(
        rows, weight, (((1,), (1,)), ((), ())), preferred_element_type=jnp.float32
    )


def sparse_body(tokens, expert_ids, route_weights, gate_weight, up_weight, down_weight):
    devices_wide = lax.axis_size("expert")
    experts = devices_wide // 2
    tok_count = expert_ids.shape[0]
    per_token = expert_ids.shape[1]
    capacity = min(tok_count, tok_count * per_token // experts)
    slot_count = experts * capacity
    arrived_count = devices_wide * capacity
    expert_range = jnp.arange(experts, dtype=jnp.int32)
    onehot = jnp.sum(
        (expert_ids[:, :, None] == expert_range[None, None, :]).astype(jnp.int32), axis=1
    )
    earlier_count = jnp.cumsum(onehot, axis=0) - onehot
    slot_rank = jnp.take_along_axis(earlier_count, expert_ids, axis=1)
    slot_of = expert_ids * capacity + slot_rank
    slot_range = jnp.arange(slot_count, dtype=jnp.int32)
    select = jnp.any(slot_of[None, :, :] == slot_range[:, None, None], axis=2).astype(jnp.bfloat16)
    weight_gate = gate_weight[0]
    weight_up = up_weight[0]
    weight_out = down_weight[0]
    whole_rows = lax.all_gather(tokens, "tensor", axis=1, tiled=True)
    packed = jnp.dot(select, whole_rows, preferred_element_type=jnp.float32).astype(jnp.bfloat16)
    packed = packed.reshape(experts, capacity, whole_rows.shape[1])
    arrived = lax.all_to_all(
        jnp.repeat(packed, 2, axis=0), "expert", split_axis=0, concat_axis=0, tiled=True
    ).reshape(arrived_count, -1)
    gate_act = rows_times(arrived, weight_gate)
    up_act = rows_times(arrived, weight_up)
    hidden = (jax.nn.silu(gate_act) * up_act).astype(jnp.bfloat16)
    columns = lax.all_to_all(weight_out, "tensor", split_axis=1, concat_axis=0, tiled=True)
    unit_count = hidden.shape[1]
    shard_piece = lax.all_gather(hidden, "tensor", axis=1, tiled=True)
    groups = shard_piece.shape[1] // unit_count
    weight_rows = columns
    weight_rows = weight_rows.reshape(groups, unit_count, columns.shape[1])
    grouped = shard_piece.reshape(shard_piece.shape[0], groups, unit_count)
    group_terms = jnp.einsum(
        "rgf,gfd->grd", grouped, weight_rows, preferred_element_type=jnp.float32
    ).astype(jnp.bfloat16)
    group_terms = lax.optimization_barrier(group_terms)
    half_out = jnp.sum(group_terms.astype(jnp.float32), axis=0).astype(jnp.bfloat16)
    returned = lax.all_to_all(
        half_out.reshape(devices_wide, capacity, -1),
        "expert",
        split_axis=0,
        concat_axis=0,
        tiled=True,
    )
    returned = returned.reshape(experts, 2, capacity, -1).astype(jnp.float32)
    combined = (returned[:, 0] + returned[:, 1]).reshape(slot_count, -1)
    picked = combined[slot_of]
    mixed_out = jnp.sum(route_weights[:, :, None] * picked, axis=1)
    return mixed_out.astype(jnp.bfloat16)


def fused_kernel(
    nz, tok_hbm, ids_ref, rw_ref, gate_hbm, up_hbm, down_hbm, out_ref,
    rows_a, rows_b, gate, up, down, part, core_buf, x_buf, y_buf, z_buf,
    load_sem, row_sem, az_send, ax_send, ay_send, ac_send,
    core_send, core_recv, x_send, x_recv, y_send, y_recv, z_send, z_recv,
):
    me, y = lax.axis_index("expert"), lax.axis_index("tensor")
    c = lax.rem(me, 2)
    x = lax.rem(me // 2, 2)
    z = me // 4
    oc, ox, oy = 1 - c, 1 - x, 1 - y
    tok, wide = out_ref.shape
    half = wide // 2
    blocks = 2 * nz
    count = 2 * blocks * tok
    experts = blocks
    top = ids_ref.shape[0]
    rows = (rows_a, rows_b)

    def dev(zz, xx, cc, yy):
        return ((zz * 2 + xx) * 2 + cc, yy)

    dev_x, dev_y, dev_c = dev(z, ox, c, y), dev(z, x, c, oy), dev(z, x, oc, y)

    def remote(src, dst, send, recv, to):
        return pltpu.make_async_remote_copy(
            src_ref=src, dst_ref=dst, send_sem=send, recv_sem=recv,
            device_id=to, device_id_type=pl.DeviceIdType.MESH,
        )

    loads = [
        pltpu.make_async_copy(src.at[0], dst, load_sem.at[i])
        for i, (src, dst) in enumerate(((gate_hbm, gate), (up_hbm, up), (down_hbm, down)))
    ]
    own = x * nz + z
    mine_a, mine_b = rows_a.at[y, c, own, :, pl.ds(0, half)], rows_b.at[y, c, own]
    tok_loads = [
        pltpu.make_async_copy(tok_hbm.at[:, pl.ds(0, half)], mine_a, load_sem.at[3]),
        pltpu.make_async_copy(tok_hbm.at[:, pl.ds(half, half)], mine_b, load_sem.at[4]),
    ]
    for load in tok_loads + loads:
        load.start()
    ids = ids_ref[...].astype(jnp.float32).T
    weights = rw_ref[...].T
    lane = lax.broadcasted_iota(jnp.int32, (tok, LANES), 1)
    which = lax.rem(lane, experts).astype(jnp.float32)
    spread = jnp.zeros((tok, LANES), jnp.float32)
    for j in range(top):
        spread = jnp.where(ids[:, j : j + 1] == which, weights[:, j : j + 1], spread)
    first = spread.astype(jnp.bfloat16).astype(jnp.float32)
    rest = spread - first
    second = rest.astype(jnp.bfloat16).astype(jnp.float32)
    third = rest - second
    parts = jnp.where(lane < experts, first, jnp.where(lane < 2 * experts, second, third))
    parts = jnp.where(lane < 3 * experts, parts, 0.0)
    rows_a[y, c, own, :, half:] = parts.astype(jnp.bfloat16)

    def other(k):
        m = nz - 1 - z
        low = k + (k >= z).astype(jnp.int32)
        high = nz - 1 - k - (k >= m).astype(jnp.int32)
        return jnp.where(z < nz // 2, low, high)

    others = [other(k) for k in range(nz - 1)]
    barrier = pltpu.get_barrier_semaphore()
    for to in [dev(zz, x, c, y) for zz in others] + [dev_x, dev_y, dev_c]:
        pl.semaphore_signal(barrier, inc=1, device_id=to, device_id_type=pl.DeviceIdType.MESH)
    for load in tok_loads:
        load.wait()
    pl.semaphore_wait(barrier, nz + 2)

    def row_copy(h, yy, cc, xx, zz, send, to):
        at = (yy, cc, xx * nz + zz)
        return remote(rows[h].at[at], rows[h].at[at], send, row_sem.at[(h,) + at], to)

    def z_copy(h, zz):
        return row_copy(h, y, c, x, z, az_send.at[h, zz], dev(zz, x, c, y))

    def x_copy(h, yy, zz):
        return row_copy(h, yy, c, x, zz, ax_send.at[h, yy, zz], dev_x)

    def y_copy(h, xx, zz):
        return row_copy(h, y, c, xx, zz, ay_send.at[h, xx, zz], dev_y)

    def c_copy(h, yy, xx, zz):
        return row_copy(h, yy, c, xx, zz, ac_send.at[h, yy, xx * nz + zz], dev_c)

    def got(h, yy, xx, zz):
        c_copy(h, yy, xx, zz).wait_recv()

    def got_forward(h, yy, xx, zz):
        got(h, yy, xx, zz)
        c_copy(h, yy, xx, zz).start()

    def column_sends(zz):
        x_copy(0, y, zz).start()
        y_copy(1, x, zz).start()
        y_copy(0, x, zz).start()
        x_copy(1, y, zz).start()
        c_copy(0, y, x, zz).start()
        c_copy(1, y, x, zz).start()

    def second_sends(zz):
        got(0, y, ox, zz)
        y_copy(0, ox, zz).start()
        c_copy(0, y, ox, zz).start()
        got(1, oy, x, zz)
        x_copy(1, oy, zz).start()
        c_copy(1, oy, x, zz).start()

    for zz in others:
        for h in range(2):
            z_copy(h, zz).start()
    column_sends(z)
    near = [z] + others
    for k in range(1, nz):
        for h in range(2):
            got(h, y, x, near[k])
        column_sends(near[k])
        second_sends(near[k - 1])
    second_sends(near[nz - 1])

    def from_core(h, yy):
        def step(k, carry):
            at = (yy, oc, k)
            remote(rows[h].at[at], rows[h].at[at], ac_send.at[h, yy, k], row_sem.at[(h,) + at], dev_c).wait_recv()
            return carry

        lax.fori_loop(0, blocks, step, 0)

    contract = (((1,), (1,)), ((), ()))

    def quarter(h, yy):
        block = rows[h][yy, :, :, :, :half].reshape(count, half)
        cols = pl.ds(pl.multiple_of((2 * yy + h) * half, LANES), half)
        g = lax.dot_general(block, gate[:, cols], contract, preferred_element_type=jnp.float32)
        u = lax.dot_general(block, up[:, cols], contract, preferred_element_type=jnp.float32)
        return g, u

    for zz in near:
        got_forward(1, y, ox, zz)
        got_forward(0, oy, x, zz)
    loads[0].wait()
    loads[1].wait()
    from_core(0, y)
    gate_0, up_0 = quarter(0, y)
    for zz in near[: nz // 2]:
        got_forward(0, oy, ox, zz)
        got_forward(1, oy, ox, zz)
    from_core(1, y)
    gate_1, up_1 = quarter(1, y)
    for zz in near[nz // 2 :]:
        got_forward(0, oy, ox, zz)
        got_forward(1, oy, ox, zz)
    from_core(0, oy)
    gate_2, up_2 = quarter(0, oy)
    from_core(1, oy)
    gate_3, up_3 = quarter(1, oy)
    gate_act = gate_0 + gate_1 + gate_2 + gate_3
    up_act = up_0 + up_1 + up_2 + up_3
    lanes = lax.broadcasted_iota(jnp.int32, (count, LANES), 1)
    mine = (lax.rem(lanes, experts) == me // 2) & (lanes < 3 * experts)
    kept = rows_a[0, :, :, :, half:].reshape(count, LANES).astype(jnp.float32)
    scale = jnp.sum(jnp.where(mine, kept, 0.0), axis=1, keepdims=True)
    hidden = (jax.nn.silu(gate_act) * up_act * scale).astype(jnp.bfloat16)
    loads[2].wait()

    def core_copy(yy, h):
        return remote(
            part.at[yy, h, oc], core_buf.at[yy, h], core_send.at[yy, h], core_recv.at[yy, h], dev_c
        )

    def rx(h, yy, zz):
        return remote(
            part.at[yy, h, c, ox * nz + zz], x_buf.at[h, yy, zz], x_send.at[h, yy, zz], x_recv.at[h, yy, zz], dev_x
        )

    def ry(h, xx, zz):
        return remote(
            part.at[oy, h, c, xx * nz + zz], y_buf.at[h, xx, zz], y_send.at[h, xx, zz], y_recv.at[h, xx, zz], dev_y
        )

    def rz(h, zz, source):
        return remote(
            part.at[y, h, c, x * nz + zz], z_buf.at[h, source], z_send.at[h, zz], z_recv.at[h, source],
            dev(zz, x, c, y),
        )

    wide_f = jnp.float32

    def project(yy, h):
        base = (2 * yy + h) * half
        piece = 256

        def down_step(k, carry):
            cols = pl.ds(pl.multiple_of(base + k * piece, 128), piece)
            got_cols = pl.ds(pl.multiple_of(k * piece, 128), piece)
            term = jnp.dot(hidden, down[:, cols], preferred_element_type=jnp.float32)
            part[yy, h, :, :, :, got_cols] = term.astype(jnp.bfloat16).reshape(2, blocks, tok, piece)
            return carry

        lax.fori_loop(0, half // piece, down_step, 0)
        core_copy(yy, h).start()

    def absorb(yy, h):
        core_copy(yy, h).wait_recv()

        def add_core(k, carry):
            total = part[yy, h, c, k].astype(wide_f) + core_buf[yy, h, k].astype(wide_f)
            part[yy, h, c, k] = total.astype(jnp.bfloat16)
            return carry

        lax.fori_loop(0, blocks, add_core, 0)

    order = [lax.rem(z + nz - 1 - k, nz) for k in range(nz)]

    def first_y(zz):
        ry(0, ox, zz).start()
        ry(0, x, zz).start()

    project(oy, 0)
    project(oy, 1)
    absorb(oy, 0)
    for zz in order[:2]:
        first_y(zz)
    project(y, 1)
    absorb(oy, 1)
    for zz in order[:2]:
        rx(1, oy, zz).start()
    project(y, 0)
    absorb(y, 1)
    for zz in order[:2]:
        rx(1, y, zz).start()
    absorb(y, 0)

    def turn(zz):
        at = ox * nz + zz
        ry(0, ox, zz).wait_recv()
        part[y, 0, c, at] = (part[y, 0, c, at].astype(wide_f) + y_buf[0, ox, zz].astype(wide_f)).astype(jnp.bfloat16)
        rx(0, y, zz).start()
        at = x * nz + zz
        rx(1, oy, zz).wait_recv()
        part[oy, 1, c, at] = (part[oy, 1, c, at].astype(wide_f) + x_buf[1, oy, zz].astype(wide_f)).astype(jnp.bfloat16)
        ry(1, x, zz).start()

    def column_sum(h, zz):
        ry(h, x, zz).wait_recv()
        rx(h, y, zz).wait_recv()
        return (
            part[y, h, c, x * nz + zz].astype(wide_f) + y_buf[h, x, zz].astype(wide_f) + x_buf[h, y, zz].astype(wide_f)
        )

    def home(zz):
        for h in range(2):
            part[y, h, c, x * nz + zz] = column_sum(h, zz).astype(jnp.bfloat16)
            rz(h, zz, z).start()

    for k in range(nz):
        turn(order[k])
        if k + 2 < nz:
            first_y(order[k + 2])
            rx(1, oy, order[k + 2]).start()
            rx(1, y, order[k + 2]).start()
        if k > 0:
            home(order[k - 1])
    for h in range(2):
        total = column_sum(h, z)
        for zz in others:
            rz(h, z, zz).wait_recv()
            total = total + z_buf[h, zz].astype(wide_f)
        out_ref[:, h * half : (h + 1) * half] = total.astype(jnp.bfloat16)

    for zz in others:
        for h in range(2):
            z_copy(h, zz).wait_send()
            rz(h, zz, z).wait_send()

    def drain(zz, carry):
        for h in range(2):
            for yy in range(2):
                for xx in range(2):
                    c_copy(h, yy, xx, zz).wait_send()
        x_copy(0, y, zz).wait_send()
        y_copy(1, x, zz).wait_send()
        rx(0, y, zz).wait_send()
        ry(1, x, zz).wait_send()
        for i in range(2):
            x_copy(1, i, zz).wait_send()
            y_copy(0, i, zz).wait_send()
            rx(1, i, zz).wait_send()
            ry(0, i, zz).wait_send()
        return carry

    lax.fori_loop(0, nz, drain, 0)
    for yy in range(2):
        for h in range(2):
            core_copy(yy, h).wait_send()


def fused_body(tokens, expert_ids, route_weights, gate_weight, up_weight, down_weight):
    nz = lax.axis_size("expert") // 4
    tok, wide = tokens.shape
    half = wide // 2
    blocks = 2 * nz
    bf16 = jnp.bfloat16
    held = gate_weight.shape[1:]
    vmem = pl.BlockSpec(memory_space=pltpu.VMEM)
    anywhere = pl.BlockSpec(memory_space=pl.ANY)
    sems = pltpu.SemaphoreType.DMA
    return pl.pallas_call(
        functools.partial(fused_kernel, nz),
        out_shape=jax.ShapeDtypeStruct((tok, wide), bf16),
        in_specs=[anywhere, vmem, vmem] + [anywhere] * 3,
        out_specs=vmem,
        scratch_shapes=[
            pltpu.VMEM((2, 2, blocks, tok, half + LANES), bf16),
            pltpu.VMEM((2, 2, blocks, tok, half), bf16),
            pltpu.VMEM(held, bf16),
            pltpu.VMEM(held, bf16),
            pltpu.VMEM(held, bf16),
            pltpu.VMEM((2, 2, 2, blocks, tok, half), bf16),
            pltpu.VMEM((2, 2, blocks, tok, half), bf16),
            pltpu.VMEM((2, 2, nz, tok, half), bf16),
            pltpu.VMEM((2, 2, nz, tok, half), bf16),
            pltpu.VMEM((2, nz, tok, half), bf16),
            sems((5,)),
            sems((2, 2, 2, blocks)),
            sems((2, nz)),
            sems((2, 2, nz)),
            sems((2, 2, nz)),
            sems((2, 2, blocks)),
            sems((2, 2)),
            sems((2, 2)),
        ]
        + [sems((2, 2, nz))] * 4
        + [sems((2, nz))] * 2,
        compiler_params=pltpu.CompilerParams(
            collective_id=0, has_side_effects=True, vmem_limit_bytes=60 * 2**20
        ),
    )(tokens, expert_ids.T, route_weights.T, gate_weight, up_weight, down_weight)


def body(*args):
    every = args[1].shape[1] == lax.axis_size("expert") // 2
    tok, wide = args[0].shape
    even = lax.axis_size("tensor") == 2 and lax.axis_size("expert") % 8 == 0
    fits = tok % 16 == 0 and wide % 512 == 0 and 3 * args[1].shape[1] <= LANES
    if every and even and fits:
        return fused_body(*args)
    return sparse_body(*args)


def solution(mesh):
    placed = (
        P("expert", "tensor"),
        P("expert", None),
        P("expert", None),
        P("expert", "tensor", None),
        P("expert", "tensor", None),
        P("expert", "tensor", None),
    )
    return jax.shard_map(
        body, mesh=mesh, in_specs=placed, out_specs=P("expert", "tensor"), check_vma=False
    )
```

```python
import functools

import jax
import jax.numpy as jnp
from jax import lax
from jax.experimental import pallas as pl
from jax.experimental.pallas import tpu as pltpu
from jax.sharding import PartitionSpec as P

LANES = 128


def rows_times(rows, weight):
    return lax.dot_general(
        rows, weight, (((1,), (1,)), ((), ())), preferred_element_type=jnp.float32
    )


def sparse_body(tokens, expert_ids, route_weights, gate_weight, up_weight, down_weight):
    devices_wide = lax.axis_size("expert")
    experts = devices_wide // 2
    tok_count = expert_ids.shape[0]
    per_token = expert_ids.shape[1]
    capacity = min(tok_count, tok_count * per_token // experts)
    slot_count = experts * capacity
    arrived_count = devices_wide * capacity
    expert_range = jnp.arange(experts, dtype=jnp.int32)
    onehot = jnp.sum(
        (expert_ids[:, :, None] == expert_range[None, None, :]).astype(jnp.int32), axis=1
    )
    earlier_count = jnp.cumsum(onehot, axis=0) - onehot
    slot_rank = jnp.take_along_axis(earlier_count, expert_ids, axis=1)
    slot_of = expert_ids * capacity + slot_rank
    slot_range = jnp.arange(slot_count, dtype=jnp.int32)
    select = jnp.any(slot_of[None, :, :] == slot_range[:, None, None], axis=2).astype(jnp.bfloat16)
    weight_gate = gate_weight[0]
    weight_up = up_weight[0]
    weight_out = down_weight[0]
    whole_rows = lax.all_gather(tokens, "tensor", axis=1, tiled=True)
    packed = jnp.dot(select, whole_rows, preferred_element_type=jnp.float32).astype(jnp.bfloat16)
    packed = packed.reshape(experts, capacity, whole_rows.shape[1])
    arrived = lax.all_to_all(
        jnp.repeat(packed, 2, axis=0), "expert", split_axis=0, concat_axis=0, tiled=True
    ).reshape(arrived_count, -1)
    gate_act = rows_times(arrived, weight_gate)
    up_act = rows_times(arrived, weight_up)
    hidden = (jax.nn.silu(gate_act) * up_act).astype(jnp.bfloat16)
    columns = lax.all_to_all(weight_out, "tensor", split_axis=1, concat_axis=0, tiled=True)
    unit_count = hidden.shape[1]
    shard_piece = lax.all_gather(hidden, "tensor", axis=1, tiled=True)
    groups = shard_piece.shape[1] // unit_count
    weight_rows = columns
    weight_rows = weight_rows.reshape(groups, unit_count, columns.shape[1])
    grouped = shard_piece.reshape(shard_piece.shape[0], groups, unit_count)
    group_terms = jnp.einsum(
        "rgf,gfd->grd", grouped, weight_rows, preferred_element_type=jnp.float32
    ).astype(jnp.bfloat16)
    group_terms = lax.optimization_barrier(group_terms)
    half_out = jnp.sum(group_terms.astype(jnp.float32), axis=0).astype(jnp.bfloat16)
    returned = lax.all_to_all(
        half_out.reshape(devices_wide, capacity, -1),
        "expert",
        split_axis=0,
        concat_axis=0,
        tiled=True,
    )
    returned = returned.reshape(experts, 2, capacity, -1).astype(jnp.float32)
    combined = (returned[:, 0] + returned[:, 1]).reshape(slot_count, -1)
    picked = combined[slot_of]
    mixed_out = jnp.sum(route_weights[:, :, None] * picked, axis=1)
    return mixed_out.astype(jnp.bfloat16)


def fused_kernel(
    nz, tok_hbm, ids_ref, rw_ref, gate_hbm, up_hbm, down_hbm, out_ref,
    rows_a, rows_b, gate, up, down, part, core_buf, x_buf, y_buf, z_buf,
    load_sem, row_sem, az_send, ax_send, ay_send, ac_send,
    core_send, core_recv, x_send, x_recv, y_send, y_recv, z_send, z_recv,
):
    me, y = lax.axis_index("expert"), lax.axis_index("tensor")
    c = lax.rem(me, 2)
    x = lax.rem(me // 2, 2)
    z = me // 4
    oc, ox, oy = 1 - c, 1 - x, 1 - y
    tok, wide = out_ref.shape
    half = wide // 2
    blocks = 2 * nz
    count = 2 * blocks * tok
    experts = blocks
    top = ids_ref.shape[0]
    rows = (rows_a, rows_b)

    def dev(zz, xx, cc, yy):
        return ((zz * 2 + xx) * 2 + cc, yy)

    dev_x, dev_y, dev_c = dev(z, ox, c, y), dev(z, x, c, oy), dev(z, x, oc, y)

    def remote(src, dst, send, recv, to):
        return pltpu.make_async_remote_copy(
            src_ref=src, dst_ref=dst, send_sem=send, recv_sem=recv,
            device_id=to, device_id_type=pl.DeviceIdType.MESH,
        )

    loads = [
        pltpu.make_async_copy(src.at[0], dst, load_sem.at[i])
        for i, (src, dst) in enumerate(((gate_hbm, gate), (up_hbm, up), (down_hbm, down)))
    ]
    own = x * nz + z
    mine_a, mine_b = rows_a.at[y, c, own, :, pl.ds(0, half)], rows_b.at[y, c, own]
    tok_loads = [
        pltpu.make_async_copy(tok_hbm.at[:, pl.ds(0, half)], mine_a, load_sem.at[3]),
        pltpu.make_async_copy(tok_hbm.at[:, pl.ds(half, half)], mine_b, load_sem.at[4]),
    ]
    for load in tok_loads + loads:
        load.start()
    ids = ids_ref[...].astype(jnp.float32).T
    weights = rw_ref[...].T
    lane = lax.broadcasted_iota(jnp.int32, (tok, LANES), 1)
    which = lax.rem(lane, experts).astype(jnp.float32)
    spread = jnp.zeros((tok, LANES), jnp.float32)
    for j in range(top):
        spread = jnp.where(ids[:, j : j + 1] == which, weights[:, j : j + 1], spread)
    first = spread.astype(jnp.bfloat16).astype(jnp.float32)
    rest = spread - first
    second = rest.astype(jnp.bfloat16).astype(jnp.float32)
    third = rest - second
    parts = jnp.where(lane < experts, first, jnp.where(lane < 2 * experts, second, third))
    parts = jnp.where(lane < 3 * experts, parts, 0.0)
    rows_a[y, c, own, :, half:] = parts.astype(jnp.bfloat16)

    def other(k):
        m = nz - 1 - z
        low = k + (k >= z).astype(jnp.int32)
        high = nz - 1 - k - (k >= m).astype(jnp.int32)
        return jnp.where(z < nz // 2, low, high)

    others = [other(k) for k in reversed(range(nz - 1))]
    barrier = pltpu.get_barrier_semaphore()
    for to in [dev(zz, x, c, y) for zz in others] + [dev_x, dev_y, dev_c]:
        pl.semaphore_signal(barrier, inc=1, device_id=to, device_id_type=pl.DeviceIdType.MESH)
    for load in tok_loads:
        load.wait()
    pl.semaphore_wait(barrier, nz + 2)

    def row_copy(h, yy, cc, xx, zz, send, to):
        at = (yy, cc, xx * nz + zz)
        return remote(rows[h].at[at], rows[h].at[at], send, row_sem.at[(h,) + at], to)

    def z_copy(h, zz):
        return row_copy(h, y, c, x, z, az_send.at[h, zz], dev(zz, x, c, y))

    def x_copy(h, yy, zz):
        return row_copy(h, yy, c, x, zz, ax_send.at[h, yy, zz], dev_x)

    def y_copy(h, xx, zz):
        return row_copy(h, y, c, xx, zz, ay_send.at[h, xx, zz], dev_y)

    def c_copy(h, yy, xx, zz):
        return row_copy(h, yy, c, xx, zz, ac_send.at[h, yy, xx * nz + zz], dev_c)

    def got(h, yy, xx, zz):
        c_copy(h, yy, xx, zz).wait_recv()

    def got_forward(h, yy, xx, zz):
        got(h, yy, xx, zz)
        c_copy(h, yy, xx, zz).start()

    def column_sends(zz):
        x_copy(0, y, zz).start()
        y_copy(1, x, zz).start()
        y_copy(0, x, zz).start()
        x_copy(1, y, zz).start()
        c_copy(0, y, x, zz).start()
        c_copy(1, y, x, zz).start()

    def second_sends(zz):
        got(0, y, ox, zz)
        y_copy(0, ox, zz).start()
        c_copy(0, y, ox, zz).start()
        got(1, oy, x, zz)
        x_copy(1, oy, zz).start()
        c_copy(1, oy, x, zz).start()

    for zz in others:
        for h in range(2):
            z_copy(h, zz).start()
    column_sends(z)
    near = [z] + others
    for k in range(1, nz):
        for h in range(2):
            got(h, y, x, near[k])
        column_sends(near[k])
        second_sends(near[k - 1])
    second_sends(near[nz - 1])

    def from_core(h, yy):
        def step(k, carry):
            at = (yy, oc, k)
            remote(rows[h].at[at], rows[h].at[at], ac_send.at[h, yy, k], row_sem.at[(h,) + at], dev_c).wait_recv()
            return carry

        lax.fori_loop(0, blocks, step, 0)

    contract = (((1,), (1,)), ((), ()))

    def quarter(h, yy):
        block = rows[h][yy, :, :, :, :half].reshape(count, half)
        cols = pl.ds(pl.multiple_of((2 * yy + h) * half, LANES), half)
        g = lax.dot_general(block, gate[:, cols], contract, preferred_element_type=jnp.float32)
        u = lax.dot_general(block, up[:, cols], contract, preferred_element_type=jnp.float32)
        return g, u

    for zz in near:
        got_forward(1, y, ox, zz)
        got_forward(0, oy, x, zz)
    loads[0].wait()
    loads[1].wait()
    from_core(0, y)
    gate_0, up_0 = quarter(0, y)
    for zz in near[: nz // 2]:
        got_forward(0, oy, ox, zz)
        got_forward(1, oy, ox, zz)
    from_core(1, y)
    gate_1, up_1 = quarter(1, y)
    for zz in near[nz // 2 :]:
        got_forward(0, oy, ox, zz)
        got_forward(1, oy, ox, zz)
    from_core(0, oy)
    gate_2, up_2 = quarter(0, oy)
    from_core(1, oy)
    gate_3, up_3 = quarter(1, oy)
    gate_act = gate_0 + gate_1 + gate_2 + gate_3
    up_act = up_0 + up_1 + up_2 + up_3
    lanes = lax.broadcasted_iota(jnp.int32, (count, LANES), 1)
    mine = (lax.rem(lanes, experts) == me // 2) & (lanes < 3 * experts)
    kept = rows_a[0, :, :, :, half:].reshape(count, LANES).astype(jnp.float32)
    scale = jnp.sum(jnp.where(mine, kept, 0.0), axis=1, keepdims=True)
    hidden = (jax.nn.silu(gate_act) * up_act * scale).astype(jnp.bfloat16)
    loads[2].wait()

    def core_copy(yy, h):
        return remote(
            part.at[yy, h, oc], core_buf.at[yy, h], core_send.at[yy, h], core_recv.at[yy, h], dev_c
        )

    def rx(h, yy, zz):
        return remote(
            part.at[yy, h, c, ox * nz + zz], x_buf.at[h, yy, zz], x_send.at[h, yy, zz], x_recv.at[h, yy, zz], dev_x
        )

    def ry(h, xx, zz):
        return remote(
            part.at[oy, h, c, xx * nz + zz], y_buf.at[h, xx, zz], y_send.at[h, xx, zz], y_recv.at[h, xx, zz], dev_y
        )

    def rz(h, zz, source):
        return remote(
            part.at[y, h, c, x * nz + zz], z_buf.at[h, source], z_send.at[h, zz], z_recv.at[h, source],
            dev(zz, x, c, y),
        )

    wide_f = jnp.float32

    def project(yy, h):
        base = (2 * yy + h) * half
        piece = 256

        def down_step(k, carry):
            cols = pl.ds(pl.multiple_of(base + k * piece, 128), piece)
            got_cols = pl.ds(pl.multiple_of(k * piece, 128), piece)
            term = jnp.dot(hidden, down[:, cols], preferred_element_type=jnp.float32)
            part[yy, h, :, :, :, got_cols] = term.astype(jnp.bfloat16).reshape(2, blocks, tok, piece)
            return carry

        lax.fori_loop(0, half // piece, down_step, 0)
        core_copy(yy, h).start()

    def absorb(yy, h):
        core_copy(yy, h).wait_recv()

        def add_core(k, carry):
            total = part[yy, h, c, k].astype(wide_f) + core_buf[yy, h, k].astype(wide_f)
            part[yy, h, c, k] = total.astype(jnp.bfloat16)
            return carry

        lax.fori_loop(0, blocks, add_core, 0)

    order = others + [z]

    def first_y(zz):
        ry(0, ox, zz).start()
        ry(0, x, zz).start()

    project(oy, 0)
    project(oy, 1)
    absorb(oy, 0)
    for zz in order[:2]:
        first_y(zz)
    project(y, 1)
    absorb(oy, 1)
    for zz in order[:2]:
        rx(1, oy, zz).start()
    project(y, 0)
    absorb(y, 1)
    for zz in order[:2]:
        rx(1, y, zz).start()
    absorb(y, 0)

    def turn(zz):
        at = ox * nz + zz
        ry(0, ox, zz).wait_recv()
        part[y, 0, c, at] = (part[y, 0, c, at].astype(wide_f) + y_buf[0, ox, zz].astype(wide_f)).astype(jnp.bfloat16)
        rx(0, y, zz).start()
        at = x * nz + zz
        rx(1, oy, zz).wait_recv()
        part[oy, 1, c, at] = (part[oy, 1, c, at].astype(wide_f) + x_buf[1, oy, zz].astype(wide_f)).astype(jnp.bfloat16)
        ry(1, x, zz).start()

    def column_sum(h, zz):
        ry(h, x, zz).wait_recv()
        rx(h, y, zz).wait_recv()
        return (
            part[y, h, c, x * nz + zz].astype(wide_f) + y_buf[h, x, zz].astype(wide_f) + x_buf[h, y, zz].astype(wide_f)
        )

    def home(zz):
        for h in range(2):
            part[y, h, c, x * nz + zz] = column_sum(h, zz).astype(jnp.bfloat16)
            rz(h, zz, z).start()

    for k in range(nz):
        turn(order[k])
        if k + 2 < nz:
            first_y(order[k + 2])
            rx(1, oy, order[k + 2]).start()
            rx(1, y, order[k + 2]).start()
        if k > 0:
            home(order[k - 1])
    for h in range(2):
        total = column_sum(h, z)
        for zz in others:
            rz(h, z, zz).wait_recv()
            total = total + z_buf[h, zz].astype(wide_f)
        out_ref[:, h * half : (h + 1) * half] = total.astype(jnp.bfloat16)

    for zz in others:
        for h in range(2):
            z_copy(h, zz).wait_send()
            rz(h, zz, z).wait_send()

    def drain(zz, carry):
        for h in range(2):
            for yy in range(2):
                for xx in range(2):
                    c_copy(h, yy, xx, zz).wait_send()
        x_copy(0, y, zz).wait_send()
        y_copy(1, x, zz).wait_send()
        rx(0, y, zz).wait_send()
        ry(1, x, zz).wait_send()
        for i in range(2):
            x_copy(1, i, zz).wait_send()
            y_copy(0, i, zz).wait_send()
            rx(1, i, zz).wait_send()
            ry(0, i, zz).wait_send()
        return carry

    lax.fori_loop(0, nz, drain, 0)
    for yy in range(2):
        for h in range(2):
            core_copy(yy, h).wait_send()


def fused_body(tokens, expert_ids, route_weights, gate_weight, up_weight, down_weight):
    nz = lax.axis_size("expert") // 4
    tok, wide = tokens.shape
    half = wide // 2
    blocks = 2 * nz
    bf16 = jnp.bfloat16
    held = gate_weight.shape[1:]
    vmem = pl.BlockSpec(memory_space=pltpu.VMEM)
    anywhere = pl.BlockSpec(memory_space=pl.ANY)
    sems = pltpu.SemaphoreType.DMA
    return pl.pallas_call(
        functools.partial(fused_kernel, nz),
        out_shape=jax.ShapeDtypeStruct((tok, wide), bf16),
        in_specs=[anywhere, vmem, vmem] + [anywhere] * 3,
        out_specs=vmem,
        scratch_shapes=[
            pltpu.VMEM((2, 2, blocks, tok, half + LANES), bf16),
            pltpu.VMEM((2, 2, blocks, tok, half), bf16),
            pltpu.VMEM(held, bf16),
            pltpu.VMEM(held, bf16),
            pltpu.VMEM(held, bf16),
            pltpu.VMEM((2, 2, 2, blocks, tok, half), bf16),
            pltpu.VMEM((2, 2, blocks, tok, half), bf16),
            pltpu.VMEM((2, 2, nz, tok, half), bf16),
            pltpu.VMEM((2, 2, nz, tok, half), bf16),
            pltpu.VMEM((2, nz, tok, half), bf16),
            sems((5,)),
            sems((2, 2, 2, blocks)),
            sems((2, nz)),
            sems((2, 2, nz)),
            sems((2, 2, nz)),
            sems((2, 2, blocks)),
            sems((2, 2)),
            sems((2, 2)),
        ]
        + [sems((2, 2, nz))] * 4
        + [sems((2, nz))] * 2,
        compiler_params=pltpu.CompilerParams(
            collective_id=0, has_side_effects=True, vmem_limit_bytes=60 * 2**20
        ),
    )(tokens, expert_ids.T, route_weights.T, gate_weight, up_weight, down_weight)


def body(*args):
    every = args[1].shape[1] == lax.axis_size("expert") // 2
    tok, wide = args[0].shape
    even = lax.axis_size("tensor") == 2 and lax.axis_size("expert") % 8 == 0
    fits = tok % 16 == 0 and wide % 512 == 0 and 3 * args[1].shape[1] <= LANES
    if every and even and fits:
        return fused_body(*args)
    return sparse_body(*args)


def solution(mesh):
    placed = (
        P("expert", "tensor"),
        P("expert", None),
        P("expert", None),
        P("expert", "tensor", None),
        P("expert", "tensor", None),
        P("expert", "tensor", None),
    )
    return jax.shard_map(
        body, mesh=mesh, in_specs=placed, out_specs=P("expert", "tensor"), check_vma=False
    )
```
